256 devices in a mesh: arc: 4 (over x), row: 16 (over z, y_lo), col: 4 (over y_hi, core).
Axes of the slice: x: 4, y: 4 (y_hi: 2, y_lo: 2; y = y_hi * 2 + y_lo), z: 8, core: 2. Of those that a mesh axis runs over, the one named last changes fastest.
Arguments:
- local_normal: float32 [4, 512, 512], P('arc', None, 'col'), may hold values from -1 to 4, as said below
- link_block: float32 [4, 7424, 512], P('arc', 'row', 'col'), may hold values from -0.5 to 0.5
- local_rhs: float32 [4, 512], P('arc', 'col'), may hold values from -6 to 6
- arc_of_slot: int32 [4], P('arc'), may hold values from 0 to 3, each once
- live_params: int32 [4], replicated, may hold values from 256 to 512
Outputs:
- elimination_term: float32 [7424, 7424], P(('arc', 'col'), 'row')
- rhs_term: float32 [7424], P('row')
The draws below stay inside these ranges and needn't reach their ends.
Inputs may be any that keep to these rules, and one draw needn't show every extreme that they name: `local_normal`: each slot's matrix is symmetric positive definite. `arc_of_slot`: each arc is held by exactly one slot.
All inputs are finite; a program needn't handle non-finite values.
Results may differ from the reference program's by a relative error of at most 0.0003.
Values sent between devices are 32-bit elements; how exact they have to be, the bound alone decides.
A program may use at most 64 MiB of HBM per device.

```python
import math
import jax
import jax.numpy as jnp
from jax import lax

G = 7424
L = 512
ARCS = 4


def draw_local_normal(key, part):
    first, second = jax.random.split(key)
    noise = jax.random.normal(first, (ARCS, L, L), jnp.float32)
    symmetric = (noise + jnp.swapaxes(noise, 1, 2)) * (0.25 / math.sqrt(L))
    diagonal = jax.random.uniform(second, (ARCS, L), jnp.float32, 1.2, 3.0)
    return symmetric + diagonal[:, :, None] * jnp.eye(L, dtype=jnp.float32)[None, :, :]


def set_ends(array, key, least, top_value):
    extent = array.shape
    place = [jax.random.randint(jax.random.fold_in(key, axis), (), 0, extent[axis]) for axis in range(len(extent))]
    array = array.at[tuple(place)].set(least)
    longest = extent.index(max(extent))
    place[longest] = (place[longest] + 1) % extent[longest]
    return array.at[tuple(place)].set(top_value)


def block_levels(own_key, shape, pieces, smallest, high):
    gain, own = 1.0, jax.random.fold_in(own_key, 6)
    for axis_at, shards_of in pieces:
        steps = jnp.exp(jax.random.uniform(jax.random.fold_in(own, axis_at), (shards_of,), jnp.float32, smallest / len(pieces), high / len(pieces)))
        gain = gain * jnp.repeat(steps, shape[axis_at] // shards_of).reshape([-1 if axis == axis_at else 1 for axis in range(len(shape))])
    return gain


def normal_values(stream_key, shape, deviation, reach, cuts=(), kind=jnp.bfloat16):
    entries = deviation * jax.random.normal(stream_key, shape, jnp.float32)
    if cuts:
        entries = entries * block_levels(stream_key, shape, cuts, -0.22, 0.18)
    return jnp.clip(entries, -reach, reach).astype(kind)


def setup_inputs(seed: int = 0) -> dict:
    streams_of = jax.random.split(jax.random.key(seed), 6)
    local_normal = draw_local_normal(jax.random.fold_in(streams_of[5], 71), 0)
    link_block = normal_values(streams_of[1], (ARCS, G, L), (L // 4) ** -0.5, 0.5, ((0, 4), (1, 16), (2, 4)), jnp.float32)
    local_rhs = normal_values(streams_of[2], (ARCS, L), 1.0, 6.0, ((0, 4), (1, 4)), jnp.float32)
    arc_of_slot = jax.random.permutation(streams_of[3], ARCS).astype(jnp.int32)
    live_params = set_ends(jax.random.randint(streams_of[4], (ARCS,), L // 2, L + 1), jax.random.fold_in(streams_of[4], 1), L // 2, L).astype(jnp.int32)
    return dict(local_normal=local_normal, link_block=link_block, local_rhs=local_rhs, arc_of_slot=arc_of_slot, live_params=live_params)


def mask_slot(normal, link, rhs, live):
    index = jnp.arange(L, dtype=jnp.int32)
    keep = (index < live).astype(jnp.float32)
    normal = normal * keep[:, None] * keep[None, :] + jnp.diag(1.0 - keep)
    return (normal, link * keep[None, :], rhs * keep)

def reference(local_normal, link_block, local_rhs, arc_of_slot, live_params):

    def add_slot(carry, items):
        total, rhs_total = carry
        normal, link, rhs, arc = items
        live = live_params[arc]
        normal, link, rhs = mask_slot(normal, link, rhs, live)
        factor = jnp.linalg.cholesky(normal)
        reduced = jax.scipy.linalg.solve_triangular(factor, link.T, lower=True).T
        solved = jax.scipy.linalg.solve_triangular(factor, rhs, lower=True)
        total = total + jnp.dot(reduced, reduced.T, precision=lax.Precision.HIGHEST)
        rhs_total = rhs_total + jnp.dot(reduced, solved, precision=lax.Precision.HIGHEST)
        return ((total, rhs_total), None)
    start = (jnp.zeros((G, G), jnp.float32), jnp.zeros((G,), jnp.float32))
    (total, rhs_total), unused = lax.scan(add_slot, start, (local_normal, link_block, local_rhs, arc_of_slot))
    return (total, rhs_total)
```

```python
import functools

import jax
import jax.numpy as jnp
from jax import lax
from jax.experimental import pallas as pl
from jax.experimental.pallas import tpu as pltpu
from jax.sharding import PartitionSpec as P

HI = lax.Precision.HIGHEST
F32 = jnp.float32
BF16 = jnp.bfloat16
UNITS = 2


def small_inverse(cols):
    s = lax.broadcasted_iota(jnp.int32, (1, 8, 128), 1)
    j = lax.broadcasted_iota(jnp.int32, (8, 1, 1), 0)
    for k in range(8):
        p = 1.0 / cols[k : k + 1, k : k + 1, :]
        f = jnp.where(j == k, p, cols[:, k : k + 1, :] * p)
        ck = jnp.where(s == k, -1.0, cols[k : k + 1])
        cols = jnp.where((s == k) | (j == k), 0.0, cols) - ck * f
    return cols


def block_inverse(a, tick):
    n = 128
    lane = lax.broadcasted_iota(jnp.int32, (1, n), 1)
    for g in range(n // 8):
        k = 8 * g
        rows = a[k : k + 8, :]
        cols = jnp.stack(
            [jnp.broadcast_to(rows[:, k + j : k + j + 1], (8, n)) for j in range(8)]
        )
        inv = small_inverse(cols)
        q = inv[0] * rows[0:1, :]
        for j in range(1, 8):
            q = q + inv[j] * rows[j : j + 1, :]
        for j in range(8):
            q = jnp.where(lane == k + j, inv[j], q)
        rest = jnp.where((lane >= k) & (lane < k + 8), 0.0, a)
        for j in range(8):
            rest = rest - a[:, k + j : k + j + 1] * q[j : j + 1, :]
        parts = [q]
        if k:
            parts.insert(0, rest[:k])
        if k + 8 < n:
            parts.append(rest[k + 8 :])
        a = jnp.concatenate(parts, 0)
        tick()
    return a


def invert(work, tick):
    for g in range(4):
        ks = slice(128 * g, 128 * g + 128)
        p = block_inverse(work[g, ks, :], tick)
        rows = [
            p
            if c == g
            else jnp.dot(p, work[c, ks, :], precision=HI, preferred_element_type=F32)
            for c in range(4)
        ]
        for t in range(4):
            if t == g:
                continue
            ts = slice(128 * t, 128 * t + 128)
            a = work[g, ts, :]
            for c in range(4):
                d = jnp.dot(a, rows[c], precision=HI, preferred_element_type=F32)
                work[c, ts, :] = -d if c == g else work[c, ts, :] - d
        for c in range(4):
            work[c, ks, :] = rows[c]


def split(v):
    high = v.astype(BF16)
    return high, (v - high.astype(F32)).astype(BF16)


def dot3(a, b, dims):
    ah, al = a
    bh, bl = b
    dn = (dims, ((), ()))
    return (
        lax.dot_general(ah, bh, dn, preferred_element_type=F32)
        + lax.dot_general(ah, bl, dn, preferred_element_type=F32)
        + lax.dot_general(al, bh, dn, preferred_element_type=F32)
    )


def kernel(
    arc_ref, live_ref, n_ref, l_ref, r_ref, out_ref, rhs_ref,
    panels, rpanels, work, ja, jb, ia, ib, inv, ah, al, bh, bl, nh, nl, wh, wl, tile, other,
    n_send, n_recv, r_send, r_recv, j_send, j_recv, jp_send, jp_recv,
    z_send, z_recv, ip_send, ip_recv, v_send, v_recv, vp_send, vp_recv, t_send, t_recv, local,
):
    x = lax.axis_index("arc")
    row = lax.axis_index("row")
    col = lax.axis_index("col")
    z, l = lax.div(row, 2), lax.rem(row, 2)
    h, b = lax.div(col, 2), lax.rem(col, 2)
    y = 2 * h + l
    home = 2 * x + h
    rows = l_ref.shape[0]
    part = rows // UNITS

    def device(dx=0, dy=0, dz=0, db=0):
        yy = lax.rem(y + dy + 4, 4)
        zz = lax.rem(z + dz + 8, 8)
        bb = lax.rem(b + db, 2)
        return {
            "arc": lax.rem(x + dx + 4, 4),
            "row": 2 * zz + lax.rem(yy, 2),
            "col": 2 * lax.div(yy, 2) + bb,
        }

    def remote(src, dst, ss, rs, dev):
        return pltpu.make_async_remote_copy(
            src_ref=src, dst_ref=dst, send_sem=ss, recv_sem=rs,
            device_id=dev, device_id_type=pl.DeviceIdType.MESH,
        )

    here = {"arc": x, "row": row, "col": col}
    swap_to = {"arc": x, "row": 2 * z + (1 - l), "col": 2 * h + (1 - b)}
    partner = device(db=1)

    barrier = pltpu.get_barrier_semaphore()
    peers = [device(dx=d) for d in (1, 2, 3)] + [device(dy=d) for d in (1, 2, 3)]
    peers += [device(dz=1), device(dz=7), partner, swap_to]
    for p in peers:
        pl.semaphore_signal(barrier, inc=1, device_id=p, device_id_type=pl.DeviceIdType.MESH)
    pl.semaphore_wait(barrier, len(peers))

    own_c = col
    far_c = 2 * (1 - h) + b
    mate_c = 2 * h + (1 - b)
    last_c = 2 * (1 - h) + (1 - b)

    def n_copy(i, slot, dev):
        return remote(panels.at[slot], panels.at[slot], n_send.at[i], n_recv.at[i], dev)

    def r_copy(i, slot, dev):
        return remote(rpanels.at[slot], rpanels.at[slot], r_send.at[i], r_recv.at[i], dev)

    def along(e, d):
        return e * (1 - b) + d * b, e * b + d * (1 - b)

    def slot_of(dx, dy):
        return lax.rem(x - dx + 8, 4), lax.rem(y - dy + 8, 4)

    def j_first(e):
        dx, dy = along(e, 0)
        return remote(l_ref, ja.at[x, y], j_send.at[e], j_recv.at[e * 4], device(dx, dy))

    def j_second(e, d):
        sx, sy = slot_of(*along(e, 0))
        dx, dy = along(0, d)
        src = l_ref if e == 0 else ja.at[sx, sy]
        return remote(src, ja.at[sx, sy], j_send.at[4 + e * 4 + d], j_recv.at[e * 4 + d], device(dx, dy))

    def j_wait(e, d):
        dx, dy = along(e, d)
        sx, sy = slot_of(dx, dy)
        remote(l_ref, ja.at[sx, sy], j_send.at[0], j_recv.at[e * 4 + d], here).wait_recv()

    def jp_copy(sx, sy):
        return remote(
            ja.at[sx, sy], jb.at[sx, lax.div(sy, 2)],
            jp_send.at[sx, lax.div(sy, 2)], jp_recv.at[sx, lax.div(sy, 2)], partner,
        )

    def j_pass(e, d):
        sx, sy = slot_of(*along(e, d))

        @pl.when(lax.rem(sy, 2) != b)
        def _():
            jp_copy(sx, sy).start()

    t_up = lax.rem(z - home + 8, 8)
    t_down = lax.rem(home - z + 8, 8)
    n_units = 4 * UNITS

    def z_slot(up, n):
        p, u = lax.div(n, UNITS), lax.rem(n, UNITS)
        dx = lax.rem(p, 2) if up else 3 - lax.rem(p, 2)
        dy = 2 * lax.div(p, 2)
        sx, sy = slot_of(dx, dy)
        return sx, lax.div(sy, 2), sy, pl.ds(u * part, part)

    def z_copy(up, n, source):
        sx, sh, sy, cut = z_slot(up, n)
        src = ja.at[sx, sy, cut] if source else ia.at[sx, sh, cut]
        k = 0 if up else 1
        return remote(
            src, ia.at[sx, sh, cut], z_send.at[k, n], z_recv.at[k, n], device(dz=1 if up else 7)
        )

    def z_step(up, m):
        t = t_up if up else t_down
        n = m - t

        @pl.when((n >= 0) & (n < n_units))
        def _():
            @pl.when(t == 0)
            def _():
                z_copy(up, n, True).start()

            @pl.when(t > 0)
            def _():
                z_copy(up, n, False).wait_recv()

                @pl.when(t < 7)
                def _():
                    z_copy(up, n, False).start()

    def i_local(sx, sh):
        return pltpu.make_async_copy(ja.at[sx, 2 * sh + l], ia.at[sx, sh], local.at[sx, sh])

    def ip_copy(sx, sh):
        return remote(ia.at[sx, sh], ib.at[sx, sh], ip_send.at[sx, sh], ip_recv.at[sx, sh], partner)

    own_local = pltpu.make_async_copy(l_ref, ja.at[x, y], local.at[4, 0])
    own_local.start()
    panels[own_c] = n_ref[...]
    rpanels[own_c] = r_ref[...]
    to_far = remote(n_ref, panels.at[own_c], n_send.at[0], n_recv.at[0], device(dy=2))
    to_mate = remote(n_ref, panels.at[own_c], n_send.at[1], n_recv.at[1], partner)
    rto_far = remote(r_ref, rpanels.at[own_c], r_send.at[0], r_recv.at[0], device(dy=2))
    rto_mate = remote(r_ref, rpanels.at[own_c], r_send.at[1], r_recv.at[1], partner)
    for c in (to_far, rto_far, to_mate, rto_mate):
        c.start()
    for e in (1, 3, 2):
        j_first(e).start()
    for d in (1, 3, 2):
        j_second(0, d).start()

    n_copy(0, far_c, here).wait_recv()
    r_copy(0, far_c, here).wait_recv()
    n_copy(2, far_c, partner).start()
    r_copy(2, far_c, partner).start()
    own_local.wait()
    n_copy(1, mate_c, here).wait_recv()
    r_copy(1, mate_c, here).wait_recv()
    n_copy(2, last_c, here).wait_recv()
    r_copy(2, last_c, here).wait_recv()

    live = live_ref[arc_ref[0]]
    sub = lax.broadcasted_iota(jnp.int32, (512, 128), 0)
    lane = lax.broadcasted_iota(jnp.int32, (512, 128), 1)
    for c in range(4):
        ident = jnp.where(sub == lane + 128 * c, 1.0, 0.0)
        keep = (sub < live) & (lane + 128 * c < live)
        work[c] = jnp.where(keep, panels[c], ident)

    events = []
    for e in (1, 3, 2):
        def first_arrival(e=e):
            j_wait(e, 0)
            for d in (1, 3, 2):
                j_second(e, d).start()
        events.append(first_arrival)

    waited = {(0, 0), (1, 0), (2, 0), (3, 0)}
    for m in range(n_units + 7):
        if m % UNITS == 0 and m // UNITS < 4:
            p = m // UNITS
            for dx in (p % 2, 3 - p % 2):
                dy = 2 * (p // 2)
                def arrive(dx=dx, dy=dy):
                    if (dx, dy) not in waited:
                        @pl.when(b == 0)
                        def _():
                            remote(l_ref, ja.at[0, 0], j_send.at[0], j_recv.at[dx * 4 + dy], here).wait_recv()
                    if (dy, dx) not in waited:
                        @pl.when(b == 1)
                        def _():
                            remote(l_ref, ja.at[0, 0], j_send.at[0], j_recv.at[dy * 4 + dx], here).wait_recv()

                events.append(arrive)

        def ring(m=m):
            z_step(True, m)
            z_step(False, m)

        events.append(ring)

    state = {"ticks": 0, "done": 0}

    def tick():
        state["ticks"] += 1
        if state["ticks"] % 2 == 0 and state["done"] < len(events):
            events[state["done"]]()
            state["done"] += 1

    invert(work, tick)
    while state["done"] < len(events):
        events[state["done"]]()
        state["done"] += 1

    v = [jnp.zeros((8, 128), F32) for _ in range(4)]
    for c in range(4):
        keep = (sub < live) & (lane + 128 * c < live)
        w = jnp.where(keep, work[c], 0.0)
        inv[x, c, 0:512, :] = w
        for t in range(4):
            r8 = jnp.broadcast_to(rpanels[t], (8, 128))
            v[c] = v[c] + jnp.dot(
                r8, w[128 * t : 128 * t + 128, :], precision=HI, preferred_element_type=F32
            )
    for c in range(4):
        inv[x, c, 512:520, :] = v[c]

    half = pl.ds(2 * b, 2)
    rest = pl.ds(2 * (1 - b), 2)

    def v_copy(d):
        return remote(inv.at[x, half], inv.at[x, half], v_send.at[d], v_recv.at[d], device(dx=d))

    def v_arrive(d):
        s = lax.rem(x - d + 4, 4)
        return remote(inv.at[s, half], inv.at[s, half], v_send.at[0], v_recv.at[d], here)

    def v_pass(d):
        s = lax.rem(x - d + 4, 4)
        return remote(inv.at[s, half], inv.at[s, half], vp_send.at[d], vp_recv.at[d], partner)

    def v_passed(d):
        s = lax.rem(x - d + 4, 4)
        return remote(inv.at[s, rest], inv.at[s, rest], vp_send.at[0], vp_recv.at[d], here)

    for d in (1, 3, 2):
        v_copy(d).start()

    order0 = {(p % 2, 2 * (p // 2)) for p in range(4)} | {(3 - p % 2, 2 * (p // 2)) for p in range(4)}
    for e in range(4):
        for d in range(4):
            if (e, d) in waited:
                continue

            @pl.when((b == 0) & ((e, d) not in order0) | (b == 1) & ((d, e) not in order0))
            def _():
                j_wait(e, d)

    for sx in range(4):
        for sh in range(2):
            @pl.when(z == home)
            def _():
                i_local(sx, sh).start()

            jp_copy(sx, 2 * sh + (1 - b)).start()
    for sx in range(4):
        for sh in range(2):
            @pl.when(z == home)
            def _():
                i_local(sx, sh).wait()

            ip_copy(sx, sh).start()
    for sx in range(4):
        for sh in range(2):
            remote(ja.at[sx, 0], jb.at[sx, sh], jp_send.at[0, 0], jp_recv.at[sx, sh], here).wait_recv()
            remote(ja.at[sx, 0], ib.at[sx, sh], ip_send.at[0, 0], ip_recv.at[sx, sh], here).wait_recv()

    tile[...] = jnp.zeros_like(tile)
    chunk = [2 * 0 + b, 2 * 1 + b, 2 * 0 + (1 - b), 2 * 1 + (1 - b)]

    for d in (0, 1, 3, 2):
        s = lax.rem(x - d + 4, 4)
        if d:
            v_arrive(d).wait_recv()
            v_pass(d).start()
            v_passed(d).wait_recv()
        for p in range(4):
            at = slice(128 * p, 128 * p + 128)
            src_i = ia if p < 2 else ib
            high, low = split(src_i[s, p % 2])
            ah[:, at], al[:, at] = high, low
            src_j = ja[s, 2 * p + b] if p < 2 else jb[s, p - 2]
            high, low = split(src_j)
            bh[:, at], bl[:, at] = high, low
            for q in range(4):
                to = slice(128 * q, 128 * q + 128)
                high, low = split(inv[s, chunk[q], pl.ds(128 * chunk[p], 128), :])
                nh[at, to], nl[at, to] = high, low
        w = dot3((ah[...], al[...]), (nh[...], nl[...]), ((1,), (0,)))
        high, low = split(w)
        wh[0:rows], wl[0:rows] = high, low
        for q in range(4):
            to = slice(128 * q, 128 * q + 128)
            high, low = split(jnp.broadcast_to(inv[s, chunk[q], 512:513, :], (16, 128)))
            wh[rows : rows + 16, to], wl[rows : rows + 16, to] = high, low
        tile[...] += dot3((wh[...], wl[...]), (bh[...], bl[...]), ((1,), (1,)))

    swap = remote(tile, other, t_send.at[0], t_recv.at[0], swap_to)
    big = lambda src: pltpu.make_async_copy(src.at[0:rows], out_ref, local.at[4, 0])
    little = lambda src: pltpu.make_async_copy(src.at[rows : rows + 8], rhs_ref, local.at[4, 1])

    @pl.when(l != b)
    def _():
        swap.start()
        swap.wait()
        big(other).start()
        little(other).start()
        big(other).wait()
        little(other).wait()

    @pl.when(l == b)
    def _():
        big(tile).start()
        little(tile).start()
        big(tile).wait()
        little(tile).wait()

    to_far.wait_send()
    to_mate.wait_send()
    rto_far.wait_send()
    rto_mate.wait_send()
    n_copy(2, far_c, partner).wait_send()
    r_copy(2, far_c, partner).wait_send()
    for e in (1, 2, 3):
        j_first(e).wait_send()
    for e in range(4):
        for d in (1, 2, 3):
            j_second(e, d).wait_send()
    for sx in range(4):
        for sh in range(2):
            jp_copy(sx, 2 * sh + (1 - b)).wait_send()
            ip_copy(sx, sh).wait_send()
    for n in range(n_units):
        for up in (True, False):
            @pl.when((t_up if up else t_down) < 7)
            def _():
                z_copy(up, n, False).wait_send()
    for d in (1, 2, 3):
        v_copy(d).wait_send()
        v_pass(d).wait_send()


def shards(local_normal, link_block, local_rhs, arc_of_slot, live_params):
    order, width = local_normal.shape[1:]
    rows = link_block.shape[1]
    vmem = pl.BlockSpec(memory_space=pltpu.VMEM)
    smem = pl.BlockSpec(memory_space=pltpu.SMEM)
    dma = pltpu.SemaphoreType.DMA
    piece = (rows, width)
    half = (4, 2) + piece
    tile, vector = pl.pallas_call(
        kernel,
        out_shape=(
            jax.ShapeDtypeStruct((rows, rows), F32),
            jax.ShapeDtypeStruct((8, rows), F32),
        ),
        in_specs=[smem, smem, vmem, vmem, vmem],
        out_specs=(pl.BlockSpec(memory_space=pl.ANY),) * 2,
        scratch_shapes=[
            pltpu.VMEM((4, order, width), F32),
            pltpu.VMEM((4, 1, width), F32),
            pltpu.VMEM((4, order, width), F32),
            pltpu.VMEM((4, 4) + piece, F32),
            pltpu.VMEM(half, F32),
            pltpu.VMEM(half, F32),
            pltpu.VMEM(half, F32),
            pltpu.VMEM((4, 4, order + 8, width), F32),
            pltpu.VMEM((rows, order), BF16),
            pltpu.VMEM((rows, order), BF16),
            pltpu.VMEM((rows, order), BF16),
            pltpu.VMEM((rows, order), BF16),
            pltpu.VMEM((order, order), BF16),
            pltpu.VMEM((order, order), BF16),
            pltpu.VMEM((rows + 16, order), BF16),
            pltpu.VMEM((rows + 16, order), BF16),
            pltpu.VMEM((rows + 16, rows), F32),
            pltpu.VMEM((rows + 16, rows), F32),
            dma((3,)), dma((3,)), dma((3,)), dma((3,)),
            dma((20,)), dma((16,)), dma((4, 2)), dma((4, 2)),
            dma((2, 4 * UNITS)), dma((2, 4 * UNITS)), dma((4, 2)), dma((4, 2)),
            dma((4,)), dma((4,)), dma((4,)), dma((4,)), dma((1,)), dma((1,)), dma((5, 2)),
        ],
        compiler_params=pltpu.CompilerParams(
            collective_id=0, has_side_effects=True, vmem_limit_bytes=56 * 2**20
        ),
        name="eliminate",
    )(arc_of_slot, live_params, local_normal[0], link_block[0], local_rhs)
    return tile, vector[0]


def solution(mesh):
    in_specs = (P("arc", None, "col"), P("arc", "row", "col"), P("arc", "col"), P("arc"), P())
    out_specs = (P(("arc", "col"), "row"), P("row"))
    return jax.shard_map(
        shards, mesh=mesh, in_specs=in_specs, out_specs=out_specs, check_vma=False
    )
```

```python
import functools

import jax
import jax.numpy as jnp
from jax import lax
from jax.experimental import pallas as pl
from jax.experimental.pallas import tpu as pltpu
from jax.sharding import PartitionSpec as P

HI = lax.Precision.HIGHEST
F32 = jnp.float32
BF16 = jnp.bfloat16
UNITS = 8
LAG = 4
PACK = (((0, 0), (1, 0), (2, 0), (3, 0), (3, 3)), ((1, 1), (2, 1), (3, 1), (2, 2), (3, 2)))


def small_inverse(cols):
    s = lax.broadcasted_iota(jnp.int32, (1, 8, 128), 1)
    j = lax.broadcasted_iota(jnp.int32, (8, 1, 1), 0)
    for k in range(8):
        p = 1.0 / cols[k : k + 1, k : k + 1, :]
        f = jnp.where(j == k, p, cols[:, k : k + 1, :] * p)
        ck = jnp.where(s == k, -1.0, cols[k : k + 1])
        cols = jnp.where((s == k) | (j == k), 0.0, cols) - ck * f
    return cols


def block_inverse(a, tick):
    n = 128
    lane = lax.broadcasted_iota(jnp.int32, (1, n), 1)
    for g in range(n // 8):
        k = 8 * g
        rows = a[k : k + 8, :]
        cols = jnp.stack(
            [jnp.broadcast_to(rows[:, k + j : k + j + 1], (8, n)) for j in range(8)]
        )
        inv = small_inverse(cols)
        q = inv[0] * rows[0:1, :]
        for j in range(1, 8):
            q = q + inv[j] * rows[j : j + 1, :]
        for j in range(8):
            q = jnp.where(lane == k + j, inv[j], q)
        rest = jnp.where((lane >= k) & (lane < k + 8), 0.0, a)
        for j in range(8):
            rest = rest - a[:, k + j : k + j + 1] * q[j : j + 1, :]
        parts = [q]
        if k:
            parts.insert(0, rest[:k])
        if k + 8 < n:
            parts.append(rest[k + 8 :])
        a = jnp.concatenate(parts, 0)
        tick()
    return a


def invert(work, tick):
    for g in range(4):
        ks = slice(128 * g, 128 * g + 128)
        p = block_inverse(work[g, ks, :], tick)
        rows = [
            p
            if c == g
            else jnp.dot(p, work[c, ks, :], precision=HI, preferred_element_type=F32)
            for c in range(4)
        ]
        for t in range(4):
            if t == g:
                continue
            ts = slice(128 * t, 128 * t + 128)
            a = work[g, ts, :]
            for c in range(4):
                d = jnp.dot(a, rows[c], precision=HI, preferred_element_type=F32)
                work[c, ts, :] = -d if c == g else work[c, ts, :] - d
        for c in range(4):
            work[c, ks, :] = rows[c]


def split(v):
    high = v.astype(BF16)
    return high, (v - high.astype(F32)).astype(BF16)


def dot3(a, b, dims):
    ah, al = a
    bh, bl = b
    dn = (dims, ((), ()))
    return (
        lax.dot_general(ah, bh, dn, preferred_element_type=F32)
        + lax.dot_general(ah, bl, dn, preferred_element_type=F32)
        + lax.dot_general(al, bh, dn, preferred_element_type=F32)
    )


def kernel(
    arc_ref, live_ref, n_ref, l_ref, r_ref, out_ref, rhs_ref,
    panels, rp, work, jj, ii, pk, ah, al, bh, bl, nh, nl, wh, wl, tile, other,
    n_send, n_recv, r_send, r_recv, rx_send, rx_recv, d_send, d_recv, j_send, j_recv,
    jp_send, jp_recv, z_send, z_recv, ip_send, ip_recv,
    v_send, v_recv, vp_send, vp_recv, t_send, t_recv, local,
):
    x = lax.axis_index("arc")
    row = lax.axis_index("row")
    col = lax.axis_index("col")
    z, l = lax.div(row, 2), lax.rem(row, 2)
    h, b = lax.div(col, 2), lax.rem(col, 2)
    y = 2 * h + l
    home = 2 * x + h
    at_home = z == home
    rows = l_ref.shape[0]

    def device(dx=0, dy=0, dz=0, db=0):
        yy = lax.rem(y + dy + 4, 4)
        zz = lax.rem(z + dz + 8, 8)
        bb = lax.rem(b + db, 2)
        return {
            "arc": lax.rem(x + dx + 4, 4),
            "row": 2 * zz + lax.rem(yy, 2),
            "col": 2 * lax.div(yy, 2) + bb,
        }

    def remote(src, dst, ss, rs, dev):
        return pltpu.make_async_remote_copy(
            src_ref=src, dst_ref=dst, send_sem=ss, recv_sem=rs,
            device_id=dev, device_id_type=pl.DeviceIdType.MESH,
        )

    here = {"arc": x, "row": row, "col": col}
    swap_to = {"arc": x, "row": 2 * z + (1 - l), "col": 2 * h + (1 - b)}
    source = {"arc": lax.div(z, 2), "row": row, "col": 2 * lax.rem(z, 2) + b}
    partner = device(db=1)

    barrier = pltpu.get_barrier_semaphore()
    peers = [device(dx=d) for d in (1, 2, 3)] + [device(dy=d) for d in (1, 2, 3)]
    peers += [device(dx=d, dy=2) for d in (1, 2, 3)]
    peers += [device(dz=1), device(dz=7), partner, swap_to]
    for p in peers:
        pl.semaphore_signal(barrier, inc=1, device_id=p, device_id_type=pl.DeviceIdType.MESH)
    pl.semaphore_wait(barrier, len(peers))

    far_c = 2 * (1 - h) + b
    mate_c = 2 * h + (1 - b)
    last_c = 2 * (1 - h) + (1 - b)

    def n_own(i, dev):
        return remote(n_ref, panels.at[col], n_send.at[i], n_recv.at[i], dev)

    def n_copy(i, slot, dev):
        return remote(panels.at[slot], panels.at[slot], n_send.at[i], n_recv.at[i], dev)

    def r_own(i, dev):
        return remote(r_ref, rp.at[x, col], r_send.at[i], r_recv.at[i], dev)

    def r_copy(i, slot, dev):
        return remote(rp.at[x, slot], rp.at[x, slot], r_send.at[i], r_recv.at[i], dev)

    def rx_copy(d):
        return remote(rp.at[x], rp.at[x], rx_send.at[d], rx_recv.at[d], device(dx=d))

    def along(e, d):
        return e * (1 - b) + d * b, e * b + d * (1 - b)

    def slot_of(dx, dy):
        return lax.rem(x - dx + 8, 4), lax.rem(y - dy + 8, 4)

    def j_at(sx, sy):
        return jj.at[sx, 2 * lax.div(sy, 2) + b, lax.rem(sy, 2)]

    def j_first(e):
        dx, dy = along(e, 0)
        return remote(l_ref, j_at(x, y), j_send.at[e], j_recv.at[e * 4], device(dx, dy))

    def j_second(e, d):
        sx, sy = slot_of(*along(e, 0))
        dx, dy = along(0, d)
        src = l_ref if e == 0 else j_at(sx, sy)
        return remote(src, j_at(sx, sy), j_send.at[4 + e * 4 + d], j_recv.at[e * 4 + d], device(dx, dy))

    def jp_copy(sx, sh):
        at = jj.at[sx, 2 * sh + b, 1 - b]
        return remote(at, at, jp_send.at[sx, sh], jp_recv.at[sx, sh], partner)

    def j_arrive(e, d):
        dx, dy = along(e, d)
        sx, sy = slot_of(dx, dy)
        if e or d:
            remote(l_ref, j_at(sx, sy), j_send.at[0], j_recv.at[e * 4 + d], here).wait_recv()

        @pl.when(lax.rem(sy, 2) != b)
        def _():
            jp_copy(sx, lax.div(sy, 2)).start()

    t_up = lax.rem(z - home + 8, 8)
    t_down = lax.rem(home - z + 8, 8)
    n_units = 4 * UNITS
    quarter = rows // 2 // 4 // 8 * 8
    sizes = (rows // 2 - 3 * quarter, quarter, quarter, quarter)

    def z_piece(up, p):
        dx = lax.rem(p, 2) if up else 3 - lax.rem(p, 2)
        sx, sy = slot_of(dx, 2 * lax.div(p, 2))
        return sx, lax.div(sy, 2)

    def d_copy(dev):
        return remote(l_ref, ii.at[x, col], d_send.at[0], d_recv.at[x, h], dev)

    def z_copy(up, n, phase):
        p, u = lax.div(n, UNITS), lax.rem(n, UNITS)
        sx, sh = z_piece(up, p)
        start = lax.div(u, 4) * (rows // 2) + sum(sizes[:phase])
        cut = pl.ds(pl.multiple_of(start, 8), sizes[phase])
        at = ii.at[sx, 2 * sh + b, cut]
        k = 0 if up else 1
        return remote(at, at, z_send.at[k, n], z_recv.at[k, n], device(dz=1 if up else 7))

    def ip_copy(sx, sh):
        at = ii.at[sx, 2 * sh + b]
        return remote(at, at, ip_send.at[sx, sh], ip_recv.at[sx, sh], partner)

    def z_step(up, m):
        t = t_up if up else t_down
        n = m - LAG * t
        phase = m % LAG

        if m < n_units:
            @pl.when(at_home)
            def _():
                if m % UNITS == 0:
                    sx, sh = z_piece(up, m // UNITS)
                    if up and m == 0:
                        own_home.wait()
                    else:
                        remote(l_ref, ii.at[sx, 2 * sh + b], d_send.at[0], d_recv.at[sx, sh], here).wait_recv()
                    ip_copy(sx, sh).start()
                z_copy(up, jnp.int32(m), phase).start()

        if m >= LAG:
            @pl.when((t > 0) & (n >= 0) & (n < n_units))
            def _():
                z_copy(up, n, phase).wait_recv()

                @pl.when(t < 7)
                def _():
                    z_copy(up, n, phase).start()

                if phase == LAG - 1:
                    @pl.when(lax.rem(n, UNITS) == UNITS - 1)
                    def _():
                        ip_copy(*z_piece(up, lax.div(n, UNITS))).start()

    own_home = pltpu.make_async_copy(l_ref, ii.at[x, col], local.at[0])
    own_j = pltpu.make_async_copy(l_ref, j_at(x, y), local.at[1])
    own_r = pltpu.make_async_copy(r_ref, rp.at[x, col], local.at[2])
    for i, dev in ((0, device(dy=2)), (1, partner)):
        n_own(i, dev).start()
        r_own(i, dev).start()

    @pl.when(at_home)
    def _():
        own_home.start()

    source_is_me = (lax.div(z, 2) == x) & (lax.rem(z, 2) == h)

    @pl.when(~source_is_me)
    def _():
        d_copy(source).start()

    own_j.start()
    own_r.start()
    panels[col] = n_ref[...]

    @pl.when(~source_is_me)
    def _():
        d_copy(source).wait_send()

    for e in (1, 3, 2):
        j_first(e).start()
    for d in (1, 3, 2):
        j_second(0, d).start()

    early = 8
    for step in range(early):
        z_step(True, step)
        z_step(False, step)
    own_j.wait()
    own_r.wait()
    j_arrive(0, 0)

    n_own(0, here).wait_recv()
    r_own(0, here).wait_recv()
    n_copy(2, far_c, partner).start()
    r_copy(2, far_c, partner).start()
    n_own(1, here).wait_recv()
    r_own(1, here).wait_recv()
    n_copy(2, last_c, here).wait_recv()
    r_copy(2, last_c, here).wait_recv()
    for d in (1, 3, 2):
        rx_copy(d).start()

    live = live_ref[arc_ref[0]]
    sub = lax.broadcasted_iota(jnp.int32, (512, 128), 0)
    lane = lax.broadcasted_iota(jnp.int32, (512, 128), 1)
    for c in range(4):
        ident = jnp.where(sub == lane + 128 * c, 1.0, 0.0)
        keep = (sub < live) & (lane + 128 * c < live)
        work[c] = jnp.where(keep, panels[c], ident)

    def first_arrival(e):
        j_arrive(e, 0)
        for d in (1, 3, 2):
            j_second(e, d).start()

    def ring(m):
        z_step(True, m)
        z_step(False, m)

    steps = n_units + 7 * LAG
    events = [functools.partial(ring, m) for m in range(early, steps)]
    for k, e in enumerate((1, 3, 2)):
        events.insert(2 * k, functools.partial(first_arrival, e))
    state = {"ticks": 0, "done": 0}

    def tick():
        state["ticks"] += 1
        n = state["ticks"]
        if n % 2 == 0 and state["done"] < len(events):
            events[state["done"]]()
            state["done"] += 1

    invert(work, tick)

    for half in range(2):
        for k, (r, c) in enumerate(PACK[half]):
            rs = slice(128 * r, 128 * r + 128)
            keep = (sub[rs] < live) & (lane[rs] + 128 * c < live)
            pk[x, half, 128 * k : 128 * k + 128, :] = jnp.where(keep, work[c, rs, :], 0.0)

    def v_copy(d):
        return remote(pk.at[x, b], pk.at[x, b], v_send.at[d], v_recv.at[d], device(dx=d))

    def v_slot(d):
        return lax.rem(x - d + 4, 4)

    def v_arrive(d):
        at = pk.at[v_slot(d), b]
        remote(at, at, v_send.at[0], v_recv.at[d], here).wait_recv()

    def v_pass(d):
        at = pk.at[v_slot(d), b]
        return remote(at, at, vp_send.at[d], vp_recv.at[d], partner)

    def v_passed(d):
        at = pk.at[v_slot(d), 1 - b]
        remote(at, at, vp_send.at[0], vp_recv.at[d], here).wait_recv()

    for d in (1, 3, 2):
        v_copy(d).start()

    def split_j(s, c):
        at = slice(512 * s + 128 * c, 512 * s + 128 * c + 128)
        bh[:, at], bl[:, at] = split(jj[s, c, b])

    def j_passed(sx, sh):
        at = jj.at[sx, 2 * sh + (1 - b), b]
        remote(at, at, jp_send.at[0, 0], jp_recv.at[sx, sh], here).wait_recv()

    def build(s):
        for half in range(2):
            for k, (r, c) in enumerate(PACK[half]):
                block = pk[s, half, 128 * k : 128 * k + 128, :]
                rs, cs = slice(128 * r, 128 * r + 128), slice(128 * c, 128 * c + 128)
                nh[s, rs, cs], nl[s, rs, cs] = split(block)
                if r != c:
                    nh[s, cs, rs], nl[s, cs, rs] = split(block.T)

    def v_get(d):
        v_arrive(d)
        v_pass(d).start()
        rx_s = rp.at[v_slot(d)]
        remote(rx_s, rx_s, rx_send.at[0], rx_recv.at[d], here).wait_recv()

    def v_use(d):
        v_passed(d)
        build(v_slot(d))

    fill = [functools.partial(j_arrive, e, d) for e in (0, 1, 3, 2) for d in (1, 3, 2)]
    fill += [functools.partial(j_passed, sx, sh) for sx in range(4) for sh in range(2)]
    fill += [functools.partial(split_j, s, c) for s in range(4) for c in range(4)]
    fill.append(lambda: build(x))
    for d in (1, 3, 2):
        fill.append(functools.partial(v_get, d))
    for d in (1, 3, 2):
        fill.append(functools.partial(v_use, d))
    left = events[state["done"] :]
    for k, event in enumerate(left):
        event()
        for f in fill[-(-len(fill) * k // len(left)) : -(-len(fill) * (k + 1) // len(left))]:
            f()

    for sx in range(4):
        for sh in range(2):
            at = ii.at[sx, 2 * sh + (1 - b)]
            remote(at, at, ip_send.at[0, 0], ip_recv.at[sx, sh], here).wait_recv()
    for s in range(4):
        for c in range(4):
            at = slice(512 * s + 128 * c, 512 * s + 128 * c + 128)
            ah[0:rows, at], al[0:rows, at] = split(ii[s, c])
            ah[rows : rows + 16, at], al[rows : rows + 16, at] = split(
                jnp.broadcast_to(rp[s, c], (16, 128))
            )

    total = rows + 16
    parts = (slice(0, total // 2), slice(total // 2, total))

    def swap(k):
        return remote(tile.at[parts[k]], other.at[parts[k]], t_send.at[k], t_recv.at[k], swap_to)

    def out_copies(k, src):
        if k == 0:
            return [pltpu.make_async_copy(src.at[parts[0]], out_ref.at[parts[0]], local.at[3])]
        return [
            pltpu.make_async_copy(
                src.at[total // 2 : rows], out_ref.at[total // 2 : rows], local.at[4]
            ),
            pltpu.make_async_copy(src.at[rows : rows + 8], rhs_ref, local.at[5]),
        ]

    for k in range(2):
        cut = parts[k]
        for s in range(4):
            at = slice(512 * s, 512 * s + 512)
            w = dot3((ah[cut, at], al[cut, at]), (nh[s], nl[s]), ((1,), (0,)))
            wh[cut, at], wl[cut, at] = split(w)
        tile[cut] = dot3((wh[cut], wl[cut]), (bh[...], bl[...]), ((1,), (1,)))

        @pl.when(l != b)
        def _():
            swap(k).start()

        @pl.when(l == b)
        def _():
            for c in out_copies(k, tile):
                c.start()

    for k in range(2):
        @pl.when(l != b)
        def _():
            swap(k).wait()
            for c in out_copies(k, other):
                c.start()

    for k in range(2):
        for c in out_copies(k, other):
            c.wait()

    n_own(0, partner).wait_send()
    n_own(1, partner).wait_send()
    r_own(0, partner).wait_send()
    r_own(1, partner).wait_send()
    n_copy(2, far_c, partner).wait_send()
    r_copy(2, far_c, partner).wait_send()

    for e in (1, 2, 3):
        j_first(e).wait_send()
        rx_copy(e).wait_send()
    for e in range(4):
        for d in (1, 2, 3):
            j_second(e, d).wait_send()
    for sx in range(4):
        for sh in range(2):
            jp_copy(sx, sh).wait_send()
            ip_copy(sx, sh).wait_send()
    for n in range(n_units):
        for up in (True, False):
            @pl.when((t_up if up else t_down) < 7)
            def _():
                z_copy(up, jnp.int32(n), n % LAG).wait_send()
    for d in (1, 2, 3):
        v_copy(d).wait_send()
        v_pass(d).wait_send()


def shards(local_normal, link_block, local_rhs, arc_of_slot, live_params):
    order, width = local_normal.shape[1:]
    rows = link_block.shape[1]
    vmem = pl.BlockSpec(memory_space=pltpu.VMEM)
    smem = pl.BlockSpec(memory_space=pltpu.SMEM)
    dma = pltpu.SemaphoreType.DMA
    piece = (rows, width)
    wide = 4 * order
    tile, vector = pl.pallas_call(
        kernel,
        out_shape=(
            jax.ShapeDtypeStruct((rows, rows), F32),
            jax.ShapeDtypeStruct((8, rows), F32),
        ),
        in_specs=[smem, smem, vmem, vmem, vmem],
        out_specs=(pl.BlockSpec(memory_space=pl.ANY),) * 2,
        scratch_shapes=[
            pltpu.VMEM((4, order, width), F32),
            pltpu.VMEM((4, 4, 1, width), F32),
            pltpu.VMEM((4, order, width), F32),
            pltpu.VMEM((4, 4, 2) + piece, F32),
            pltpu.VMEM((4, 4) + piece, F32),
            pltpu.VMEM((4, 2, 5 * width, width), F32),
            pltpu.VMEM((rows + 16, wide), BF16),
            pltpu.VMEM((rows + 16, wide), BF16),
            pltpu.VMEM((rows, wide), BF16),
            pltpu.VMEM((rows, wide), BF16),
            pltpu.VMEM((4, order, order), BF16),
            pltpu.VMEM((4, order, order), BF16),
            pltpu.VMEM((rows + 16, wide), BF16),
            pltpu.VMEM((rows + 16, wide), BF16),
            pltpu.VMEM((rows + 16, rows), F32),
            pltpu.VMEM((rows + 16, rows), F32),
            dma((3,)), dma((3,)), dma((3,)), dma((3,)), dma((4,)), dma((4,)),
            dma((1,)), dma((4, 2)), dma((20,)), dma((16,)),
            dma((4, 2)), dma((4, 2)), dma((2, 4 * UNITS)), dma((2, 4 * UNITS)), dma((4, 2)), dma((4, 2)),
            dma((4,)), dma((4,)), dma((4,)), dma((4,)), dma((2,)), dma((2,)), dma((6,)),
        ],
        compiler_params=pltpu.CompilerParams(
            collective_id=0, has_side_effects=True, vmem_limit_bytes=56 * 2**20
        ),
        name="eliminate",
    )(arc_of_slot, live_params, local_normal[0], link_block[0], local_rhs)
    return tile, vector[0]


def solution(mesh):
    in_specs = (P("arc", None, "col"), P("arc", "row", "col"), P("arc", "col"), P("arc"), P())
    out_specs = (P(("arc", "col"), "row"), P("row"))
    return jax.shard_map(
        shards, mesh=mesh, in_specs=in_specs, out_specs=out_specs, check_vma=False
    )
```

```python
import functools

import jax
import jax.numpy as jnp
from jax import lax
from jax.experimental import pallas as pl
from jax.experimental.pallas import tpu as pltpu
from jax.sharding import PartitionSpec as P

HI = lax.Precision.HIGHEST
F32 = jnp.float32
BF16 = jnp.bfloat16
PACK = (((0, 0), (1, 0), (2, 0), (3, 0), (3, 3)), ((1, 1), (2, 1), (3, 1), (2, 2), (3, 2)))


def small_inverse(cols):
    s = lax.broadcasted_iota(jnp.int32, (1, 8, 128), 1)
    j = lax.broadcasted_iota(jnp.int32, (8, 1, 1), 0)
    for k in range(8):
        p = 1.0 / cols[k : k + 1, k : k + 1, :]
        f = jnp.where(j == k, p, cols[:, k : k + 1, :] * p)
        ck = jnp.where(s == k, -1.0, cols[k : k + 1])
        cols = jnp.where((s == k) | (j == k), 0.0, cols) - ck * f
    return cols


def block_inverse(a, tick):
    n = 128
    lane = lax.broadcasted_iota(jnp.int32, (1, n), 1)
    for g in range(n // 8):
        k = 8 * g
        rows = a[k : k + 8, :]
        cols = jnp.stack(
            [jnp.broadcast_to(rows[:, k + j : k + j + 1], (8, n)) for j in range(8)]
        )
        inv = small_inverse(cols)
        q = inv[0] * rows[0:1, :]
        for j in range(1, 8):
            q = q + inv[j] * rows[j : j + 1, :]
        for j in range(8):
            q = jnp.where(lane == k + j, inv[j], q)
        rest = jnp.where((lane >= k) & (lane < k + 8), 0.0, a)
        for j in range(8):
            rest = rest - a[:, k + j : k + j + 1] * q[j : j + 1, :]
        parts = [q]
        if k:
            parts.insert(0, rest[:k])
        if k + 8 < n:
            parts.append(rest[k + 8 :])
        a = jnp.concatenate(parts, 0)
        tick()
    return a


def invert(work, tick):
    for g in range(4):
        ks = slice(128 * g, 128 * g + 128)
        p = block_inverse(work[g, ks, :], tick)
        rows = [
            p
            if c == g
            else jnp.dot(p, work[c, ks, :], precision=HI, preferred_element_type=F32)
            for c in range(4)
        ]
        for t in range(4):
            if t == g:
                continue
            ts = slice(128 * t, 128 * t + 128)
            a = work[g, ts, :]
            for c in range(4):
                d = jnp.dot(a, rows[c], precision=HI, preferred_element_type=F32)
                work[c, ts, :] = -d if c == g else work[c, ts, :] - d
        for c in range(4):
            work[c, ks, :] = rows[c]


def split(v):
    high = v.astype(BF16)
    return high, (v - high.astype(F32)).astype(BF16)


def dot3(a, b, dims):
    ah, al = a
    bh, bl = b
    dn = (dims, ((), ()))
    return (
        lax.dot_general(ah, bh, dn, preferred_element_type=F32)
        + lax.dot_general(ah, bl, dn, preferred_element_type=F32)
        + lax.dot_general(al, bh, dn, preferred_element_type=F32)
    )


def kernel(
    arc_ref, live_ref, n_ref, l_ref, r_ref, out_ref, rhs_ref,
    panels, rp, work, jj, zb, ii, pk, ah, al, bh, bl, nh, nl, wh, wl, tile, other,
    n_send, n_recv, r_send, r_recv, rx_send, rx_recv, j_send, j_recv,
    jp_send, jp_recv, z_send, z_recv, i_send, i_recv, ip_send, ip_recv,
    v_send, v_recv, vp_send, vp_recv, t_send, t_recv, local,
):
    x = lax.axis_index("arc")
    row = lax.axis_index("row")
    col = lax.axis_index("col")
    z, l = lax.div(row, 2), lax.rem(row, 2)
    h, b = lax.div(col, 2), lax.rem(col, 2)
    y = 2 * h + l
    home = 2 * x + h
    rows = l_ref.shape[0]

    def device(dx=0, dy=0, dz=0, db=0):
        yy = lax.rem(y + dy + 4, 4)
        zz = lax.rem(z + dz + 8, 8)
        bb = lax.rem(b + db, 2)
        return {
            "arc": lax.rem(x + dx + 4, 4),
            "row": 2 * zz + lax.rem(yy, 2),
            "col": 2 * lax.div(yy, 2) + bb,
        }

    def remote(src, dst, ss, rs, dev):
        return pltpu.make_async_remote_copy(
            src_ref=src, dst_ref=dst, send_sem=ss, recv_sem=rs,
            device_id=dev, device_id_type=pl.DeviceIdType.MESH,
        )

    here = {"arc": x, "row": row, "col": col}
    swap_to = {"arc": x, "row": 2 * z + (1 - l), "col": 2 * h + (1 - b)}
    partner = device(db=1)

    barrier = pltpu.get_barrier_semaphore()
    peers = [device(dx=d) for d in (1, 2, 3)] + [device(dy=d) for d in (1, 2, 3)]
    peers += [device(dx=d, dy=2) for d in (1, 2, 3)]
    peers += [device(dz=1), device(dz=7), partner, swap_to]
    for p in peers:
        pl.semaphore_signal(barrier, inc=1, device_id=p, device_id_type=pl.DeviceIdType.MESH)
    pl.semaphore_wait(barrier, len(peers))

    far_c = 2 * (1 - h) + b
    mate_c = 2 * h + (1 - b)
    last_c = 2 * (1 - h) + (1 - b)

    def n_own(i, dev):
        return remote(n_ref, panels.at[col], n_send.at[i], n_recv.at[i], dev)

    def n_copy(i, slot, dev):
        return remote(panels.at[slot], panels.at[slot], n_send.at[i], n_recv.at[i], dev)

    def r_own(i, dev):
        return remote(r_ref, rp.at[x, col], r_send.at[i], r_recv.at[i], dev)

    def r_copy(i, slot, dev):
        return remote(rp.at[x, slot], rp.at[x, slot], r_send.at[i], r_recv.at[i], dev)

    def rx_copy(d):
        return remote(rp.at[x], rp.at[x], rx_send.at[d], rx_recv.at[d], device(dx=d))

    def along(e, d):
        return e * (1 - b) + d * b, e * b + d * (1 - b)

    def slot_of(dx, dy):
        return lax.rem(x - dx + 8, 4), lax.rem(y - dy + 8, 4)

    def j_at(sx, sy):
        return jj.at[sx, 2 * lax.div(sy, 2) + b, lax.rem(sy, 2)]

    def j_first(e):
        dx, dy = along(e, 0)
        return remote(l_ref, j_at(x, y), j_send.at[e], j_recv.at[e * 4], device(dx, dy))

    def j_second(e, d):
        sx, sy = slot_of(*along(e, 0))
        dx, dy = along(0, d)
        src = l_ref if e == 0 else j_at(sx, sy)
        return remote(src, j_at(sx, sy), j_send.at[4 + e * 4 + d], j_recv.at[e * 4 + d], device(dx, dy))

    def jp_copy(sx, sh):
        at = jj.at[sx, 2 * sh + b, 1 - b]
        return remote(at, at, jp_send.at[sx, sh], jp_recv.at[sx, sh], partner)

    def j_arrive(e, d):
        dx, dy = along(e, d)
        sx, sy = slot_of(dx, dy)
        if e or d:
            remote(l_ref, j_at(sx, sy), j_send.at[0], j_recv.at[e * 4 + d], here).wait_recv()

        @pl.when(lax.rem(sy, 2) != b)
        def _():
            jp_copy(sx, lax.div(sy, 2)).start()

    half_rows = rows // 2

    def z_slot(up, k):
        return lax.rem(z + (8 - k if up else k), 8)

    def z_copy(up, k, part):
        q = z_slot(up, k - 1)
        cut = pl.ds(part * half_rows, half_rows)
        src = l_ref.at[cut] if k == 1 else zb.at[q, cut]
        i = 0 if up else 1
        return remote(
            src, zb.at[q, cut], z_send.at[i, k - 1, part], z_recv.at[i, k - 1, part],
            device(dz=1 if up else 7),
        )

    def z_arrive(up, k, part):
        q = z_slot(up, k)
        cut = pl.ds(part * half_rows, half_rows)
        i = 0 if up else 1
        remote(
            zb.at[q, cut], zb.at[q, cut], z_send.at[0, 0, 0], z_recv.at[i, k - 1, part], here
        ).wait_recv()
        if k < 3 or k == 3 and part == i:
            z_copy(up, k + 1, part).start()

    def i_copy(q, src):
        user = {"arc": lax.div(q, 2), "row": row, "col": 2 * lax.rem(q, 2) + b}
        return remote(src, ii.at[x, col], i_send.at[q], i_recv.at[x, h], user)

    def i_local(src):
        return pltpu.make_async_copy(src, ii.at[x, col], local.at[0])

    def i_start(q, src):
        @pl.when(q == home)
        def _():
            i_local(src).start()

        @pl.when(q != home)
        def _():
            i_copy(q, src).start()

    def ip_copy(sx, sh):
        at = ii.at[sx, 2 * sh + b]
        return remote(at, at, ip_send.at[sx, sh], ip_recv.at[sx, sh], partner)

    def i_arrive(dx, dh):
        sx, sy = slot_of(dx, 2 * dh)
        sh = lax.div(sy, 2)
        if dx or dh:
            at = ii.at[sx, 2 * sh + b]
            remote(at, at, i_send.at[0], i_recv.at[sx, sh], here).wait_recv()
        else:
            i_local(l_ref).wait()
        ip_copy(sx, sh).start()

    def z_event(k, part):
        if k < 4:
            for up in (True, False):
                z_arrive(up, k, part)
                if part:
                    i_start(z_slot(up, k), zb.at[z_slot(up, k)])
        else:
            z_arrive(True, 4, 0)
            z_arrive(False, 4, 1)
            i_start(z_slot(True, 4), zb.at[z_slot(True, 4)])

    own_j = pltpu.make_async_copy(l_ref, j_at(x, y), local.at[1])
    own_r = pltpu.make_async_copy(r_ref, rp.at[x, col], local.at[2])
    for i, dev in ((0, device(dy=2)), (1, partner)):
        n_own(i, dev).start()
        r_own(i, dev).start()

    for part in range(2):
        for up in (True, False):
            z_copy(up, 1, part).start()
    own_j.start()
    own_r.start()
    panels[col] = n_ref[...]

    for e in (1, 3, 2):
        j_first(e).start()
    for d in (1, 3, 2):
        j_second(0, d).start()

    i_start(z, l_ref)
    own_j.wait()
    own_r.wait()
    j_arrive(0, 0)
    z_event(1, 0)
    z_event(1, 1)

    n_own(0, here).wait_recv()
    r_own(0, here).wait_recv()
    n_copy(2, far_c, partner).start()
    r_copy(2, far_c, partner).start()
    n_own(1, here).wait_recv()
    r_own(1, here).wait_recv()
    n_copy(2, last_c, here).wait_recv()
    r_copy(2, last_c, here).wait_recv()
    for d in (1, 3, 2):
        rx_copy(d).start()

    live = live_ref[arc_ref[0]]
    sub = lax.broadcasted_iota(jnp.int32, (512, 128), 0)
    lane = lax.broadcasted_iota(jnp.int32, (512, 128), 1)
    for c in range(4):
        ident = jnp.where(sub == lane + 128 * c, 1.0, 0.0)
        keep = (sub < live) & (lane + 128 * c < live)
        work[c] = jnp.where(keep, panels[c], ident)

    def first_arrival(e):
        j_arrive(e, 0)
        for d in (1, 3, 2):
            j_second(e, d).start()

    events = {2 + 2 * k: functools.partial(first_arrival, e) for k, e in enumerate((1, 3, 2))}
    for n, k, part in ((12, 2, 0), (20, 2, 1), (29, 3, 0), (38, 3, 1), (52, 4, 0)):
        events[n] = functools.partial(z_event, k, part)
    state = {"ticks": 0}

    def tick():
        state["ticks"] += 1
        if state["ticks"] in events:
            events[state["ticks"]]()

    invert(work, tick)

    for half in range(2):
        for k, (r, c) in enumerate(PACK[half]):
            rs = slice(128 * r, 128 * r + 128)
            keep = (sub[rs] < live) & (lane[rs] + 128 * c < live)
            pk[x, half, 128 * k : 128 * k + 128, :] = jnp.where(keep, work[c, rs, :], 0.0)

    def v_copy(d):
        return remote(pk.at[x, b], pk.at[x, b], v_send.at[d], v_recv.at[d], device(dx=d))

    def v_slot(d):
        return lax.rem(x - d + 4, 4)

    def v_relay(d):
        length = pk.shape[2] // 2
        at = pk.at[v_slot(d), b, pl.ds(0 if d == 1 else length, length)]
        k = 0 if d == 1 else 2
        return remote(at, at, v_send.at[k], v_recv.at[k], device(dx=d))

    def v_arrive(d):
        if d == 2:
            for k in (0, 2):
                at = pk.at[v_slot(2), b, pl.ds(0, pk.shape[2] // 2)]
                remote(at, at, v_send.at[0], v_recv.at[k], here).wait_recv()
        else:
            at = pk.at[v_slot(d), b]
            remote(at, at, v_send.at[0], v_recv.at[d], here).wait_recv()
            v_relay(d).start()

    def v_pass(d):
        at = pk.at[v_slot(d), b]
        return remote(at, at, vp_send.at[d], vp_recv.at[d], partner)

    def v_passed(d):
        at = pk.at[v_slot(d), 1 - b]
        remote(at, at, vp_send.at[0], vp_recv.at[d], here).wait_recv()

    for d in (1, 3):
        v_copy(d).start()

    def split_j(s, c):
        at = slice(512 * s + 128 * c, 512 * s + 128 * c + 128)
        bh[:, at], bl[:, at] = split(jj[s, c, b])

    def j_passed(sx, sh):
        at = jj.at[sx, 2 * sh + (1 - b), b]
        remote(at, at, jp_send.at[0, 0], jp_recv.at[sx, sh], here).wait_recv()

    def build(s):
        for half in range(2):
            for k, (r, c) in enumerate(PACK[half]):
                block = pk[s, half, 128 * k : 128 * k + 128, :]
                rs, cs = slice(128 * r, 128 * r + 128), slice(128 * c, 128 * c + 128)
                nh[s, rs, cs], nl[s, rs, cs] = split(block)
                if r != c:
                    nh[s, cs, rs], nl[s, cs, rs] = split(block.T)

    def v_get(d):
        v_arrive(d)
        v_pass(d).start()
        rx_s = rp.at[v_slot(d)]
        remote(rx_s, rx_s, rx_send.at[0], rx_recv.at[d], here).wait_recv()

    def v_use(d):
        v_passed(d)
        build(v_slot(d))

    fill = [functools.partial(j_arrive, e, d) for e in (0, 1, 3, 2) for d in (1, 3, 2)]
    fill += [functools.partial(v_get, d) for d in (1, 3)]
    fill += [functools.partial(j_passed, sx, sh) for sx in range(4) for sh in range(2)]
    fill += [functools.partial(split_j, s, c) for s in range(4) for c in range(4)]
    fill.append(functools.partial(build, x))
    fill += [functools.partial(i_arrive, dx, dh) for dh in (0, 1) for dx in (0, 1, 3, 2)]
    fill.append(functools.partial(v_get, 2))
    fill += [functools.partial(v_use, d) for d in (1, 3, 2)]
    for f in fill:
        f()

    for sx in range(4):
        for sh in range(2):
            at = ii.at[sx, 2 * sh + (1 - b)]
            remote(at, at, ip_send.at[0, 0], ip_recv.at[sx, sh], here).wait_recv()
    for s in range(4):
        for c in range(4):
            at = slice(512 * s + 128 * c, 512 * s + 128 * c + 128)
            ah[0:rows, at], al[0:rows, at] = split(ii[s, c])
            ah[rows : rows + 16, at], al[rows : rows + 16, at] = split(
                jnp.broadcast_to(rp[s, c], (16, 128))
            )

    total = rows + 16
    parts = (slice(0, total // 2), slice(total // 2, total))

    def swap(k):
        return remote(tile.at[parts[k]], other.at[parts[k]], t_send.at[k], t_recv.at[k], swap_to)

    def out_copies(k, src):
        if k == 0:
            return [pltpu.make_async_copy(src.at[parts[0]], out_ref.at[parts[0]], local.at[3])]
        return [
            pltpu.make_async_copy(
                src.at[total // 2 : rows], out_ref.at[total // 2 : rows], local.at[4]
            ),
            pltpu.make_async_copy(src.at[rows : rows + 8], rhs_ref, local.at[5]),
        ]

    for k in range(2):
        cut = parts[k]
        for s in range(4):
            at = slice(512 * s, 512 * s + 512)
            w = dot3((ah[cut, at], al[cut, at]), (nh[s], nl[s]), ((1,), (0,)))
            wh[cut, at], wl[cut, at] = split(w)
        tile[cut] = dot3((wh[cut], wl[cut]), (bh[...], bl[...]), ((1,), (1,)))

        @pl.when(l != b)
        def _():
            swap(k).start()

        @pl.when(l == b)
        def _():
            for c in out_copies(k, tile):
                c.start()

    for k in range(2):
        @pl.when(l != b)
        def _():
            swap(k).wait()
            for c in out_copies(k, other):
                c.start()

    for k in range(2):
        for c in out_copies(k, other):
            c.wait()

    n_own(0, partner).wait_send()
    n_own(1, partner).wait_send()
    r_own(0, partner).wait_send()
    r_own(1, partner).wait_send()
    n_copy(2, far_c, partner).wait_send()
    r_copy(2, far_c, partner).wait_send()

    for e in (1, 2, 3):
        j_first(e).wait_send()
        rx_copy(e).wait_send()
    for e in range(4):
        for d in (1, 2, 3):
            j_second(e, d).wait_send()
    for sx in range(4):
        for sh in range(2):
            jp_copy(sx, sh).wait_send()
            ip_copy(sx, sh).wait_send()
    for up in (True, False):
        for k in (1, 2, 3, 4):
            for part in range(2):
                if k < 4 or part == (0 if up else 1):
                    z_copy(up, k, part).wait_send()
    for q in range(8):
        @pl.when(home != q)
        def _():
            i_copy(q, l_ref).wait_send()

    for d in (1, 3):
        v_copy(d).wait_send()
        v_relay(d).wait_send()
    for d in (1, 2, 3):
        v_pass(d).wait_send()


def shards(local_normal, link_block, local_rhs, arc_of_slot, live_params):
    order, width = local_normal.shape[1:]
    rows = link_block.shape[1]
    vmem = pl.BlockSpec(memory_space=pltpu.VMEM)
    smem = pl.BlockSpec(memory_space=pltpu.SMEM)
    dma = pltpu.SemaphoreType.DMA
    piece = (rows, width)
    wide = 4 * order
    tile, vector = pl.pallas_call(
        kernel,
        out_shape=(
            jax.ShapeDtypeStruct((rows, rows), F32),
            jax.ShapeDtypeStruct((8, rows), F32),
        ),
        in_specs=[smem, smem, vmem, vmem, vmem],
        out_specs=(pl.BlockSpec(memory_space=pl.ANY),) * 2,
        scratch_shapes=[
            pltpu.VMEM((4, order, width), F32),
            pltpu.VMEM((4, 4, 1, width), F32),
            pltpu.VMEM((4, order, width), F32),
            pltpu.VMEM((4, 4, 2) + piece, F32),
            pltpu.VMEM((8,) + piece, F32),
            pltpu.VMEM((4, 4) + piece, F32),
            pltpu.VMEM((4, 2, 5 * width, width), F32),
            pltpu.VMEM((rows + 16, wide), BF16),
            pltpu.VMEM((rows + 16, wide), BF16),
            pltpu.VMEM((rows, wide), BF16),
            pltpu.VMEM((rows, wide), BF16),
            pltpu.VMEM((4, order, order), BF16),
            pltpu.VMEM((4, order, order), BF16),
            pltpu.VMEM((rows + 16, wide), BF16),
            pltpu.VMEM((rows + 16, wide), BF16),
            pltpu.VMEM((rows + 16, rows), F32),
            pltpu.VMEM((rows + 16, rows), F32),
            dma((3,)), dma((3,)), dma((3,)), dma((3,)), dma((4,)), dma((4,)),
            dma((20,)), dma((16,)),
            dma((4, 2)), dma((4, 2)), dma((2, 4, 2)), dma((2, 4, 2)), dma((8,)), dma((4, 2)), dma((4, 2)), dma((4, 2)),
            dma((4,)), dma((4,)), dma((4,)), dma((4,)), dma((2,)), dma((2,)), dma((6,)),
        ],
        compiler_params=pltpu.CompilerParams(
            collective_id=0, has_side_effects=True, vmem_limit_bytes=56 * 2**20
        ),
        name="eliminate",
    )(arc_of_slot, live_params, local_normal[0], link_block[0], local_rhs)
    return tile, vector[0]


def solution(mesh):
    in_specs = (P("arc", None, "col"), P("arc", "row", "col"), P("arc", "col"), P("arc"), P())
    out_specs = (P(("arc", "col"), "row"), P("row"))
    return jax.shard_map(
        shards, mesh=mesh, in_specs=in_specs, out_specs=out_specs, check_vma=False
    )
```

```python
import functools

import jax
import jax.numpy as jnp
from jax import lax
from jax.experimental import pallas as pl
from jax.experimental.pallas import tpu as pltpu
from jax.sharding import PartitionSpec as P

HI = lax.Precision.HIGHEST
F32 = jnp.float32
BF16 = jnp.bfloat16
PACK = (((0, 0), (1, 0), (2, 0), (3, 0), (3, 3)), ((1, 1), (2, 1), (3, 1), (2, 2), (3, 2)))


def small_inverse(cols):
    s = lax.broadcasted_iota(jnp.int32, (1, 8, 128), 1)
    j = lax.broadcasted_iota(jnp.int32, (8, 1, 1), 0)
    for k in range(8):
        p = 1.0 / cols[k : k + 1, k : k + 1, :]
        f = jnp.where(j == k, p, cols[:, k : k + 1, :] * p)
        ck = jnp.where(s == k, -1.0, cols[k : k + 1])
        cols = jnp.where((s == k) | (j == k), 0.0, cols) - ck * f
    return cols


def block_inverse(a, tick):
    n = 128
    lane = lax.broadcasted_iota(jnp.int32, (1, n), 1)
    for g in range(n // 8):
        k = 8 * g
        rows = a[k : k + 8, :]
        cols = jnp.stack(
            [jnp.broadcast_to(rows[:, k + j : k + j + 1], (8, n)) for j in range(8)]
        )
        inv = small_inverse(cols)
        q = inv[0] * rows[0:1, :]
        for j in range(1, 8):
            q = q + inv[j] * rows[j : j + 1, :]
        for j in range(8):
            q = jnp.where(lane == k + j, inv[j], q)
        rest = jnp.where((lane >= k) & (lane < k + 8), 0.0, a)
        for j in range(8):
            rest = rest - a[:, k + j : k + j + 1] * q[j : j + 1, :]
        parts = [q]
        if k:
            parts.insert(0, rest[:k])
        if k + 8 < n:
            parts.append(rest[k + 8 :])
        a = jnp.concatenate(parts, 0)
        tick()
    return a


def invert(work, tick):
    for g in range(4):
        ks = slice(128 * g, 128 * g + 128)
        p = block_inverse(work[g, ks, :], tick)
        rows = [
            p
            if c == g
            else jnp.dot(p, work[c, ks, :], precision=HI, preferred_element_type=F32)
            for c in range(4)
        ]
        for t in range(4):
            if t == g:
                continue
            ts = slice(128 * t, 128 * t + 128)
            a = work[g, ts, :]
            for c in range(4):
                d = jnp.dot(a, rows[c], precision=HI, preferred_element_type=F32)
                work[c, ts, :] = -d if c == g else work[c, ts, :] - d
        for c in range(4):
            work[c, ks, :] = rows[c]


def split(v):
    high = v.astype(BF16)
    return high, (v - high.astype(F32)).astype(BF16)


def dot3(a, b, dims):
    ah, al = a
    bh, bl = b
    dn = (dims, ((), ()))
    return (
        lax.dot_general(ah, bh, dn, preferred_element_type=F32)
        + lax.dot_general(ah, bl, dn, preferred_element_type=F32)
        + lax.dot_general(al, bh, dn, preferred_element_type=F32)
    )


def kernel(
    arc_ref, live_ref, n_ref, l_ref, r_ref, out_ref, rhs_ref,
    panels, rp, work, jj, zb, ii, pk, ah, al, bh, bl, nh, nl, wh, wl, tile, other,
    n_send, n_recv, r_send, r_recv, rx_send, rx_recv, j_send, j_recv,
    jp_send, jp_recv, z_send, z_recv, i_send, i_recv, ip_send, ip_recv,
    v_send, v_recv, vp_send, vp_recv, t_send, t_recv, local,
):
    x = lax.axis_index("arc")
    row = lax.axis_index("row")
    col = lax.axis_index("col")
    z, l = lax.div(row, 2), lax.rem(row, 2)
    h, b = lax.div(col, 2), lax.rem(col, 2)
    y = 2 * h + l
    home = 2 * x + h
    rows = l_ref.shape[0]

    def device(dx=0, dy=0, dz=0, db=0):
        yy = lax.rem(y + dy + 4, 4)
        zz = lax.rem(z + dz + 8, 8)
        bb = lax.rem(b + db, 2)
        return {
            "arc": lax.rem(x + dx + 4, 4),
            "row": 2 * zz + lax.rem(yy, 2),
            "col": 2 * lax.div(yy, 2) + bb,
        }

    def remote(src, dst, ss, rs, dev):
        return pltpu.make_async_remote_copy(
            src_ref=src, dst_ref=dst, send_sem=ss, recv_sem=rs,
            device_id=dev, device_id_type=pl.DeviceIdType.MESH,
        )

    here = {"arc": x, "row": row, "col": col}
    swap_to = {"arc": x, "row": 2 * z + (1 - l), "col": 2 * h + (1 - b)}
    partner = device(db=1)

    barrier = pltpu.get_barrier_semaphore()
    peers = [device(dx=d) for d in (1, 2, 3)] + [device(dy=d) for d in (1, 2, 3)]
    peers += [device(dx=d, dy=2) for d in (1, 2, 3)]
    peers += [device(dz=1), device(dz=7), partner, swap_to]
    for p in peers:
        pl.semaphore_signal(barrier, inc=1, device_id=p, device_id_type=pl.DeviceIdType.MESH)
    pl.semaphore_wait(barrier, len(peers))

    far_c = 2 * (1 - h) + b
    mate_c = 2 * h + (1 - b)
    last_c = 2 * (1 - h) + (1 - b)

    def n_own(i, dev):
        return remote(n_ref, panels.at[col], n_send.at[i], n_recv.at[i], dev)

    def n_copy(i, slot, dev):
        return remote(panels.at[slot], panels.at[slot], n_send.at[i], n_recv.at[i], dev)

    def r_own(i, dev):
        return remote(r_ref, rp.at[x, col], r_send.at[i], r_recv.at[i], dev)

    def r_copy(i, slot, dev):
        return remote(rp.at[x, slot], rp.at[x, slot], r_send.at[i], r_recv.at[i], dev)

    def rx_copy(d):
        return remote(rp.at[x], rp.at[x], rx_send.at[d], rx_recv.at[d], device(dx=d))

    def along(e, d):
        return e * (1 - b) + d * b, e * b + d * (1 - b)

    def slot_of(dx, dy):
        return lax.rem(x - dx + 8, 4), lax.rem(y - dy + 8, 4)

    def j_at(sx, sy):
        return jj.at[sx, 2 * lax.div(sy, 2) + b, lax.rem(sy, 2)]

    def j_first(e):
        dx, dy = along(e, 0)
        return remote(l_ref, j_at(x, y), j_send.at[e], j_recv.at[e * 4], device(dx, dy))

    def j_second(e, d):
        sx, sy = slot_of(*along(e, 0))
        dx, dy = along(0, d)
        src = l_ref if e == 0 else j_at(sx, sy)
        return remote(src, j_at(sx, sy), j_send.at[4 + e * 4 + d], j_recv.at[e * 4 + d], device(dx, dy))

    def jp_copy(sx, sh):
        at = jj.at[sx, 2 * sh + b, 1 - b]
        return remote(at, at, jp_send.at[sx, sh], jp_recv.at[sx, sh], partner)

    def j_arrive(e, d):
        dx, dy = along(e, d)
        sx, sy = slot_of(dx, dy)
        if e or d:
            remote(l_ref, j_at(sx, sy), j_send.at[0], j_recv.at[e * 4 + d], here).wait_recv()

        @pl.when(lax.rem(sy, 2) != b)
        def _():
            jp_copy(sx, lax.div(sy, 2)).start()

    half_rows = rows // 2

    def z_slot(up, k):
        return lax.rem(z + (8 - k if up else k), 8)

    def z_copy(up, k, part):
        q = z_slot(up, k - 1)
        cut = pl.ds(part * half_rows, half_rows)
        src = l_ref.at[cut] if k == 1 else zb.at[q, cut]
        i = 0 if up else 1
        return remote(
            src, zb.at[q, cut], z_send.at[i, k - 1, part], z_recv.at[i, k - 1, part],
            device(dz=1 if up else 7),
        )

    def z_arrive(up, k, part):
        q = z_slot(up, k)
        cut = pl.ds(part * half_rows, half_rows)
        i = 0 if up else 1
        remote(
            zb.at[q, cut], zb.at[q, cut], z_send.at[0, 0, 0], z_recv.at[i, k - 1, part], here
        ).wait_recv()
        if k < 3 or k == 3 and part == i:
            z_copy(up, k + 1, part).start()

    def i_copy(q, src):
        user = {"arc": lax.div(q, 2), "row": row, "col": 2 * lax.rem(q, 2) + b}
        return remote(src, ii.at[x, col], i_send.at[q], i_recv.at[x, h], user)

    def i_local(src):
        return pltpu.make_async_copy(src, ii.at[x, col], local.at[0])

    def i_start(q, src):
        @pl.when(q == home)
        def _():
            i_local(src).start()

        @pl.when(q != home)
        def _():
            i_copy(q, src).start()

    def ip_copy(sx, sh):
        at = ii.at[sx, 2 * sh + b]
        return remote(at, at, ip_send.at[sx, sh], ip_recv.at[sx, sh], partner)

    def i_arrive(dx, dh):
        sx, sy = slot_of(dx, 2 * dh)
        sh = lax.div(sy, 2)
        if dx or dh:
            at = ii.at[sx, 2 * sh + b]
            remote(at, at, i_send.at[0], i_recv.at[sx, sh], here).wait_recv()
        else:
            i_local(l_ref).wait()
        ip_copy(sx, sh).start()

    def z_event(k, part):
        if k < 4:
            for up in (True, False):
                z_arrive(up, k, part)
                if part:
                    i_start(z_slot(up, k), zb.at[z_slot(up, k)])
        else:
            z_arrive(True, 4, 0)
            z_arrive(False, 4, 1)
            i_start(z_slot(True, 4), zb.at[z_slot(True, 4)])

    own_j = pltpu.make_async_copy(l_ref, j_at(x, y), local.at[1])
    own_r = pltpu.make_async_copy(r_ref, rp.at[x, col], local.at[2])
    for i, dev in ((0, device(dy=2)), (1, partner)):
        n_own(i, dev).start()
        r_own(i, dev).start()

    for part in range(2):
        for up in (True, False):
            z_copy(up, 1, part).start()
    own_j.start()
    own_r.start()
    panels[col] = n_ref[...]

    for e in (1, 3, 2):
        j_first(e).start()
    for d in (1, 3, 2):
        j_second(0, d).start()

    i_start(z, l_ref)
    own_j.wait()
    own_r.wait()
    j_arrive(0, 0)
    z_event(1, 0)
    z_event(1, 1)

    n_own(0, here).wait_recv()
    r_own(0, here).wait_recv()
    n_copy(2, far_c, partner).start()
    r_copy(2, far_c, partner).start()
    n_own(1, here).wait_recv()
    r_own(1, here).wait_recv()
    n_copy(2, last_c, here).wait_recv()
    r_copy(2, last_c, here).wait_recv()
    for d in (1, 3, 2):
        rx_copy(d).start()

    live = live_ref[arc_ref[0]]
    sub = lax.broadcasted_iota(jnp.int32, (512, 128), 0)
    lane = lax.broadcasted_iota(jnp.int32, (512, 128), 1)
    for c in range(4):
        ident = jnp.where(sub == lane + 128 * c, 1.0, 0.0)
        keep = (sub < live) & (lane + 128 * c < live)
        work[c] = jnp.where(keep, panels[c], ident)

    def first_arrival(e):
        j_arrive(e, 0)
        for d in (1, 3, 2):
            j_second(e, d).start()

    events = {2 + 2 * k: functools.partial(first_arrival, e) for k, e in enumerate((1, 3, 2))}
    for n, k, part in ((12, 2, 0), (20, 2, 1), (29, 3, 0), (38, 3, 1), (52, 4, 0)):
        events[n] = functools.partial(z_event, k, part)
    state = {"ticks": 0}

    def tick():
        state["ticks"] += 1
        if state["ticks"] in events:
            events[state["ticks"]]()

    invert(work, tick)

    for half in range(2):
        for k, (r, c) in enumerate(PACK[half]):
            rs = slice(128 * r, 128 * r + 128)
            keep = (sub[rs] < live) & (lane[rs] + 128 * c < live)
            pk[x, half, 128 * k : 128 * k + 128, :] = jnp.where(keep, work[c, rs, :], 0.0)

    def v_copy(d):
        return remote(pk.at[x, b], pk.at[x, b], v_send.at[d], v_recv.at[d], device(dx=d))

    def v_slot(d):
        return lax.rem(x - d + 4, 4)

    def v_relay(d):
        length = pk.shape[2] // 2
        at = pk.at[v_slot(d), b, pl.ds(0 if d == 1 else length, length)]
        k = 0 if d == 1 else 2
        return remote(at, at, v_send.at[k], v_recv.at[k], device(dx=d))

    def v_arrive(d):
        if d == 2:
            for k in (0, 2):
                at = pk.at[v_slot(2), b, pl.ds(0, pk.shape[2] // 2)]
                remote(at, at, v_send.at[0], v_recv.at[k], here).wait_recv()
        else:
            at = pk.at[v_slot(d), b]
            remote(at, at, v_send.at[0], v_recv.at[d], here).wait_recv()
            v_relay(d).start()

    def v_pass(d):
        at = pk.at[v_slot(d), b]
        return remote(at, at, vp_send.at[d], vp_recv.at[d], partner)

    def v_passed(d):
        at = pk.at[v_slot(d), 1 - b]
        remote(at, at, vp_send.at[0], vp_recv.at[d], here).wait_recv()

    for d in (1, 3):
        v_copy(d).start()

    def split_j(s, c):
        at = slice(512 * s + 128 * c, 512 * s + 128 * c + 128)
        bh[:, at], bl[:, at] = split(jj[s, c, b])

    def j_passed(sx, sh):
        at = jj.at[sx, 2 * sh + (1 - b), b]
        remote(at, at, jp_send.at[0, 0], jp_recv.at[sx, sh], here).wait_recv()

    def build(s):
        for half in range(2):
            for k, (r, c) in enumerate(PACK[half]):
                block = pk[s, half, 128 * k : 128 * k + 128, :]
                rs, cs = slice(128 * r, 128 * r + 128), slice(128 * c, 128 * c + 128)
                nh[s, rs, cs], nl[s, rs, cs] = split(block)
                if r != c:
                    nh[s, cs, rs], nl[s, cs, rs] = split(block.T)

    def v_get(d):
        v_arrive(d)
        v_pass(d).start()
        rx_s = rp.at[v_slot(d)]
        remote(rx_s, rx_s, rx_send.at[0], rx_recv.at[d], here).wait_recv()

    def v_use(d):
        v_passed(d)
        build(v_slot(d))

    fill = [functools.partial(j_arrive, e, d) for e in (0, 1, 3, 2) for d in (1, 3, 2)]
    fill += [functools.partial(v_get, d) for d in (1, 3)]
    fill += [functools.partial(j_passed, sx, sh) for sx in range(4) for sh in range(2)]
    fill += [functools.partial(split_j, s, c) for s in range(4) for c in range(4)]
    fill.append(functools.partial(build, x))
    fill += [functools.partial(i_arrive, dx, dh) for dh in (0, 1) for dx in (0, 1, 3, 2)]
    fill.append(functools.partial(v_get, 2))
    fill += [functools.partial(v_use, d) for d in (1, 3, 2)]
    for f in fill:
        f()

    for sx in range(4):
        for sh in range(2):
            at = ii.at[sx, 2 * sh + (1 - b)]
            remote(at, at, ip_send.at[0, 0], ip_recv.at[sx, sh], here).wait_recv()
    for s in range(4):
        for c in range(4):
            at = slice(512 * s + 128 * c, 512 * s + 128 * c + 128)
            ah[0:rows, at], al[0:rows, at] = split(ii[s, c])
            ah[rows : rows + 16, at], al[rows : rows + 16, at] = split(
                jnp.broadcast_to(rp[s, c], (16, 128))
            )

    total = rows + 16
    parts = (slice(0, total // 2), slice(total // 2, total))

    def swap(k):
        return remote(tile.at[parts[k]], other.at[parts[k]], t_send.at[k], t_recv.at[k], swap_to)

    def out_copies(k, src):
        if k == 0:
            return [pltpu.make_async_copy(src.at[parts[0]], out_ref.at[parts[0]], local.at[3])]
        return [
            pltpu.make_async_copy(
                src.at[total // 2 : rows], out_ref.at[total // 2 : rows], local.at[4]
            ),
            pltpu.make_async_copy(src.at[rows : rows + 1], rhs_ref, local.at[5]),
        ]

    for k in range(2):
        cut = parts[k]
        for s in range(4):
            at = slice(512 * s, 512 * s + 512)
            w = dot3((ah[cut, at], al[cut, at]), (nh[s], nl[s]), ((1,), (0,)))
            wh[cut, at], wl[cut, at] = split(w)
        tile[cut] = dot3((wh[cut], wl[cut]), (bh[...], bl[...]), ((1,), (1,)))

        @pl.when(l != b)
        def _():
            swap(k).start()

        @pl.when(l == b)
        def _():
            for c in out_copies(k, tile):
                c.start()

    for k in range(2):
        @pl.when(l != b)
        def _():
            swap(k).wait()
            for c in out_copies(k, other):
                c.start()

    for k in range(2):
        for c in out_copies(k, other):
            c.wait()

    n_own(0, partner).wait_send()
    n_own(1, partner).wait_send()
    r_own(0, partner).wait_send()
    r_own(1, partner).wait_send()
    n_copy(2, far_c, partner).wait_send()
    r_copy(2, far_c, partner).wait_send()

    for e in (1, 2, 3):
        j_first(e).wait_send()
        rx_copy(e).wait_send()
    for e in range(4):
        for d in (1, 2, 3):
            j_second(e, d).wait_send()
    for sx in range(4):
        for sh in range(2):
            jp_copy(sx, sh).wait_send()
            ip_copy(sx, sh).wait_send()
    for up in (True, False):
        for k in (1, 2, 3, 4):
            for part in range(2):
                if k < 4 or part == (0 if up else 1):
                    z_copy(up, k, part).wait_send()
    for q in range(8):
        @pl.when(home != q)
        def _():
            i_copy(q, l_ref).wait_send()

    for d in (1, 3):
        v_copy(d).wait_send()
        v_relay(d).wait_send()
    for d in (1, 2, 3):
        v_pass(d).wait_send()


def shards(local_normal, link_block, local_rhs, arc_of_slot, live_params):
    order, width = local_normal.shape[1:]
    rows = link_block.shape[1]
    vmem = pl.BlockSpec(memory_space=pltpu.VMEM)
    smem = pl.BlockSpec(memory_space=pltpu.SMEM)
    dma = pltpu.SemaphoreType.DMA
    piece = (rows, width)
    wide = 4 * order
    tile, vector = pl.pallas_call(
        kernel,
        out_shape=(
            jax.ShapeDtypeStruct((rows, rows), F32),
            jax.ShapeDtypeStruct((1, rows), F32),
        ),
        in_specs=[smem, smem, vmem, vmem, vmem],
        out_specs=(pl.BlockSpec(memory_space=pl.ANY),) * 2,
        scratch_shapes=[
            pltpu.VMEM((4, order, width), F32),
            pltpu.VMEM((4, 4, 1, width), F32),
            pltpu.VMEM((4, order, width), F32),
            pltpu.VMEM((4, 4, 2) + piece, F32),
            pltpu.VMEM((8,) + piece, F32),
            pltpu.VMEM((4, 4) + piece, F32),
            pltpu.VMEM((4, 2, 5 * width, width), F32),
            pltpu.VMEM((rows + 16, wide), BF16),
            pltpu.VMEM((rows + 16, wide), BF16),
            pltpu.VMEM((rows, wide), BF16),
            pltpu.VMEM((rows, wide), BF16),
            pltpu.VMEM((4, order, order), BF16),
            pltpu.VMEM((4, order, order), BF16),
            pltpu.VMEM((rows + 16, wide), BF16),
            pltpu.VMEM((rows + 16, wide), BF16),
            pltpu.VMEM((rows + 16, rows), F32),
            pltpu.VMEM((rows + 16, rows), F32),
            dma((3,)), dma((3,)), dma((3,)), dma((3,)), dma((4,)), dma((4,)),
            dma((20,)), dma((16,)),
            dma((4, 2)), dma((4, 2)), dma((2, 4, 2)), dma((2, 4, 2)), dma((8,)), dma((4, 2)), dma((4, 2)), dma((4, 2)),
            dma((4,)), dma((4,)), dma((4,)), dma((4,)), dma((2,)), dma((2,)), dma((6,)),
        ],
        compiler_params=pltpu.CompilerParams(
            collective_id=0, has_side_effects=True, vmem_limit_bytes=56 * 2**20
        ),
        name="eliminate",
    )(arc_of_slot, live_params, local_normal[0], link_block[0], local_rhs)
    return tile, vector.reshape(rows)


def solution(mesh):
    in_specs = (P("arc", None, "col"), P("arc", "row", "col"), P("arc", "col"), P("arc"), P())
    out_specs = (P(("arc", "col"), "row"), P("row"))
    return jax.shard_map(
        shards, mesh=mesh, in_specs=in_specs, out_specs=out_specs, check_vma=False
    )
```
